32 devices in a mesh: line: 2 (over core), bus: 16 (over z, y, x).
Axes of the slice: x: 2, y: 2, z: 4, core: 2. Of those that a mesh axis runs over, the one named last changes fastest.
Arguments:
- injections: float32 [64, 69632], P(None, 'bus'), may hold values from -6 to 6
- transfer_factors: float32 [4096, 69632], P('line', 'bus'), may hold values from -0.0234375 to 0.0234375
- outage_factors: float32 [4096, 8192], P('line', 'bus'), may hold values from -1 to 1
- outage_line: int32 [8192], P('bus'), may hold values from 0 to 4095
- limit_table: int32 [4, 4096], P(None, 'line'), may hold values from 1 to 4
- scenario_tier: int32 [64], replicated, may hold values from 0 to 3
Outputs:
- injection_grad: float32 [64, 69632], P('line', 'bus')
- mean_penalty: float32 [64], replicated
The draws below stay inside these ranges and needn't reach their ends.
All inputs are finite; a program needn't handle non-finite values.
Results may differ from the reference program's by a relative error of at most 0.0003.
Values sent between devices are 32-bit elements; how exact they have to be, the bound alone decides.
No kernel may reach another device: no remote copies, remote signals or barrier semaphores. Data moves between devices by JAX's collectives and lax.ppermute only.
A program may use at most 128 MiB of HBM per device.

```python
import jax
import jax.numpy as jnp
from jax import lax

BUSES = 69632
LINES = 4096
OUTAGES = 8192
TIERS = 4
SCEN = 64


def with_ends(array, rng, least, high):
    longest = array.shape.index(max(array.shape))
    spots = []
    for shift in (0, 1):
        where = [jax.random.randint(jax.random.fold_in(rng, axis), (), 0, length) for axis, length in enumerate(array.shape)]
        where[longest] = (where[longest] + shift) % array.shape[longest]
        spots.append(tuple(where))
    return array.at[spots[0]].set(least).at[spots[1]].set(high)


def levels(stream_key, extent, shards, least, high):
    gain = 1.0
    for position, blocks in shards:
        draws = jax.random.uniform(jax.random.fold_in(jax.random.fold_in(stream_key, 6), position), (blocks,), jnp.float32, least / len(shards), high / len(shards))
        gain = gain * jnp.repeat(jnp.exp(draws), extent[position] // blocks).reshape((-1,) + (1,) * (len(extent) - 1 - position))
    return gain


def centred(key, shape, spread, bound, cuts=(), dtype=jnp.bfloat16):
    array = spread * jax.random.normal(key, shape, jnp.float32)
    if cuts:
        array = array * levels(key, shape, cuts, -0.22, 0.18)
    return jnp.clip(array, -bound, bound).astype(dtype)


def setup_inputs(seed: int = 0) -> dict:
    key_of = jax.random.split(jax.random.key(seed), 7)
    injections = centred(key_of[0], (SCEN, BUSES), 1.0, 6.0, ((1, 16),), jnp.float32)
    transfer_factors = centred(key_of[1], (LINES, BUSES), BUSES ** -0.5, 0.0234375, ((0, 2), (1, 16)), jnp.float32)
    outage_factors = jnp.clip(jax.random.uniform(key_of[2], (LINES, OUTAGES), jnp.float32, -1.0, 1.0) * levels(key_of[2], (LINES, OUTAGES), ((0, 2), (1, 16)), -0.4, 0.0), -1.0, 1.0)
    outage_line = with_ends(jax.random.randint(key_of[3], (OUTAGES,), 0, LINES), jax.random.fold_in(key_of[3], 1), 0, LINES - 1).astype(jnp.int32)
    limit_table = with_ends(jax.random.randint(key_of[4], (TIERS, LINES), 1, 5), jax.random.fold_in(key_of[4], 1), 1, 4).astype(jnp.int32)
    scenario_tier = with_ends(jax.random.randint(key_of[5], (SCEN,), 0, TIERS), jax.random.fold_in(key_of[5], 1), 0, TIERS - 1).astype(jnp.int32)
    return {"injections": injections, "transfer_factors": transfer_factors, "outage_factors": outage_factors, "outage_line": outage_line, "limit_table": limit_table, "scenario_tier": scenario_tier}


def reference(injections, transfer_factors, outage_factors, outage_line, limit_table, scenario_tier):
    flows = jnp.dot(injections, transfer_factors.T, precision=lax.Precision.HIGHEST, preferred_element_type=jnp.float32)
    outage_flows = jnp.take(flows, outage_line, axis=1)
    limits = 0.4 * jnp.take(limit_table, scenario_tier, axis=0).astype(jnp.float32)

    def one_scenario(values):
        flow_row, outage_row, limit_row = values
        post = flow_row[:, None] + outage_factors * outage_row[None, :]
        excess = jnp.maximum(jnp.abs(post) - limit_row[:, None], 0.0)
        weight = 2.0 * excess * jnp.sign(post) / OUTAGES
        return jnp.sum(excess * excess), jnp.sum(weight, axis=1), jnp.sum(weight * outage_factors, axis=0)

    penalty, direct, back = lax.map(one_scenario, (flows, outage_flows, limits))
    mean_penalty = penalty / (LINES * OUTAGES)
    carried = jax.ops.segment_sum(back.T, outage_line, num_segments=LINES).T
    flow_grad = direct + carried
    injection_grad = jnp.dot(flow_grad, transfer_factors, precision=lax.Precision.HIGHEST, preferred_element_type=jnp.float32)
    return injection_grad, mean_penalty
```

```python
import functools

import jax
import jax.numpy as jnp
from jax import lax
from jax.experimental import pallas as pl
from jax.experimental.pallas import tpu as pltpu
from jax.sharding import PartitionSpec as P


F32 = jnp.float32
BF16 = jnp.bfloat16
NT = (((1,), (1,)), ((), ()))
NN = (((1,), (0,)), ((), ()))


def split(x, parts):
    pieces = []
    for _ in range(parts):
        piece = x.astype(BF16)
        pieces.append(piece)
        x = x - piece.astype(F32)
    return pieces


def tile_of(extent, most):
    best = extent
    for size in range(128, most + 1, 128):
        if extent % size == 0:
            best = size
    return best


def tree_sum(values):
    values = list(values)
    while len(values) > 1:
        values = [values[i] + values[i + 1] for i in range(0, len(values), 2)]
    return values[0]


def flow_kernel(group, tiles, index, inj_ref, factor_ref, *rest):
    outs, stacked = rest[:group], rest[group]
    scen = inj_ref.shape[0]
    step = pl.program_id(0)

    @pl.when(step == 0)
    def _():
        high, low = split(inj_ref[...], 2)
        stacked[:scen, :] = high
        stacked[scen:, :] = low

    high, low = split(factor_ref[...], 2)
    both = lax.dot_general(stacked[...], high, NT, preferred_element_type=F32)
    both += lax.dot_general(stacked[...], low, NT, preferred_element_type=F32)
    result = both[:scen] + both[scen:]
    width = result.shape[1]
    for j in range(group):
        for t in range(tiles):

            @pl.when(step == j * tiles + t)
            def _():
                outs[j][:, t * width : (t + 1) * width] = result


def partial_flows(injections, factors, group, index):
    scen, buses = injections.shape
    rows = factors.shape[0]
    block = rows // group
    tile = tile_of(block, 256)
    tiles = block // tile
    grid_spec = pltpu.PrefetchScalarGridSpec(
        num_scalar_prefetch=1,
        grid=(group * tiles,),
        in_specs=[
            pl.BlockSpec((scen, buses), lambda i, index: (0, 0)),
            pl.BlockSpec(
                (tile, buses),
                lambda i, index: ((index[0] ^ (i // tiles)) * tiles + i % tiles, 0),
            ),
        ],
        out_specs=[pl.BlockSpec((scen, block), lambda i, index: (0, 0))] * group,
        scratch_shapes=[pltpu.VMEM((2 * scen, buses), BF16)],
    )
    return pl.pallas_call(
        functools.partial(flow_kernel, group, tiles),
        grid_spec=grid_spec,
        out_shape=[jax.ShapeDtypeStruct((scen, block), F32)] * group,
        cost_estimate=pl.CostEstimate(
            flops=8 * scen * buses * rows,
            bytes_accessed=4 * buses * rows,
            transcendentals=0,
        ),
        name="partial_flows",
    )(index, injections, factors)


def chosen(index_ref, j, block, outage_row):
    rows = lax.broadcasted_iota(jnp.int32, (block, outage_row.shape[1]), 0)
    start = index_ref[1] + (index_ref[0] ^ j) * block
    return jnp.where(rows + start == outage_row, 1.0, 0.0).astype(BF16)


def pick_kernel(group, index_ref, line_ref, *rest):
    flows, out = rest[:group], rest[group]
    scen, block = flows[0].shape
    total = None
    for j in range(group):
        lhs = jnp.concatenate(split(flows[j][...], 3), axis=0)
        part = lax.dot_general(
            lhs,
            chosen(index_ref, j, block, line_ref[...]),
            NN,
            preferred_element_type=F32,
        )
        part = part[:scen] + part[scen : 2 * scen] + part[2 * scen :]
        total = part if total is None else total + part
    out[...] = total


def carry_kernel(group, backs, scale, index_ref, line_ref, *rest):
    direct = rest[:group]
    parts = rest[group : group + backs]
    outs = rest[group + backs :]
    scen, block = direct[0].shape
    back = tree_sum([part[...] for part in parts])
    lhs = jnp.concatenate(split(back[:scen], 3), axis=0)
    for j in range(group):
        part = lax.dot_general(
            lhs,
            chosen(index_ref, j, block, line_ref[...]),
            NT,
            preferred_element_type=F32,
        )
        part = part[:scen] + part[scen : 2 * scen] + part[2 * scen :]
        outs[j][:scen, :] = scale * (direct[j][...] + part)
        outs[j][scen:, :] = back[scen:, :block]


def outage_kernel(group, others, index_ref, tier_ref, *rest):
    flows = rest[:group]
    picked = rest[group : group + others]
    factor_ref, table_ref = rest[group + others : group + others + 2]
    rest = rest[group + others + 2 :]
    direct = rest[:group]
    back_ref = rest[group]
    turned, level, wide, sums, held, held_back, pen = rest[group + 1 :]
    scen, block = flows[0].shape
    outages = factor_ref.shape[1]
    lanes = 128
    cols = block // lanes
    both = 2

    for j in range(group):
        start = pl.multiple_of((index_ref[0] ^ j) * block, lanes)
        for k in range(outages // lanes):
            turned[j, k * lanes : (k + 1) * lanes, :] = factor_ref[
                pl.ds(start, block), k * lanes : (k + 1) * lanes
            ].T
        level[j] = 0.4 * table_ref[:, pl.ds(start, block)].astype(F32)

    def pair(step, carry):
        for r in range(both):
            s = step * both + r
            row = tree_sum([ref[pl.ds(s, 1), :] for ref in picked])
            for k in range(outages // lanes):
                part = row[:, k * lanes : (k + 1) * lanes]
                wide[r, k * lanes : (k + 1) * lanes, :] = jnp.broadcast_to(
                    part, (lanes, lanes)
                ).T
        squares = [jnp.zeros((8, lanes), F32) for _ in range(both)]
        for j in range(group):
            lows, highs = [], []
            for r in range(both):
                s = step * both + r
                limit = level[j, pl.ds(tier_ref[s], 1), :]
                flow = flows[j][pl.ds(s, 1), :]
                low, high = -limit - flow, limit - flow
                for c in range(cols):
                    cut = slice(c * lanes, (c + 1) * lanes)
                    lows.append(jnp.broadcast_to(low[:, cut], (8, lanes)))
                    highs.append(jnp.broadcast_to(high[:, cut], (8, lanes)))

            def body(k, state):
                state = list(state)
                at = pl.ds(pl.multiple_of(k * 8, 8), 8)
                factors = [
                    turned[j, at, c * lanes : (c + 1) * lanes] for c in range(cols)
                ]
                for r in range(both):
                    flow = wide[r, at, :]
                    total = None if j == 0 else sums[r, at, :]
                    for c in range(cols):
                        n = r * cols + c
                        q = factors[c] * flow
                        over = q - jnp.minimum(jnp.maximum(q, lows[n]), highs[n])
                        state[n] = state[n] + over
                        state[both * cols + r] = state[both * cols + r] + over * over
                        part = over * factors[c]
                        total = part if total is None else total + part
                    sums[r, at, :] = total
                return tuple(state)

            init = tuple([jnp.zeros((8, lanes), F32)] * (both * cols) + squares)
            state = lax.fori_loop(0, outages // 8, body, init, unroll=8)
            for r in range(both):
                s = step * both + r
                for c in range(cols):
                    held[j, s, :, c * lanes : (c + 1) * lanes] = state[r * cols + c]
            squares = list(state[both * cols :])
        for r in range(both):
            s = step * both + r
            pen[s] = squares[r]
            for k in range(outages // lanes):
                cut = slice(k * lanes, (k + 1) * lanes)
                held_back[s, :, cut] = jnp.sum(
                    sums[r, cut, :].T.reshape(lanes // 8, 8, lanes), axis=0
                )
        return carry

    lax.fori_loop(0, scen // both, pair, 0)

    def finish(step, carry):
        at = pl.ds(pl.multiple_of(step * 8, 8), 8)
        for j in range(group):
            direct[j][at, :] = jnp.sum(held[j, at], axis=1)
        back_ref[at, :] = jnp.sum(held_back[at], axis=1)
        return carry

    lax.fori_loop(0, scen // 8, finish, 0)
    back_ref[scen:, :] = jnp.zeros((back_ref.shape[0] - scen, outages), F32)
    back_ref[scen : scen + 1, :scen] = jnp.sum(
        jnp.sum(pen[...], axis=1).T, axis=0, keepdims=True
    )


def spread_kernel(group, lines, index_ref, *rest):
    grads = rest[:group]
    factor_ref = rest[group]
    outs = rest[group + 1 : group + 1 + lines]
    stacked = rest[group + 1 + lines]
    scen, block = grads[0].shape
    rows = scen // lines

    @pl.when(pl.program_id(0) == 0)
    def _():
        for j in range(group):
            for i in range(lines):
                at = pl.ds(pl.multiple_of((index_ref[1] ^ i) * rows, 8), rows)
                high, low = split(grads[j][at, :], 2)
                stacked[j, i * rows : (i + 1) * rows, :] = high.astype(F32)
                stacked[j, scen + i * rows : scen + (i + 1) * rows, :] = low.astype(F32)

    total = None
    for j in range(group):
        at = pl.ds(pl.multiple_of((index_ref[0] ^ j) * block, 8), block)
        lhs = stacked[j].astype(BF16)
        for part in split(factor_ref[at, :], 2):
            term = lax.dot_general(lhs, part, NN, preferred_element_type=F32)
            total = term if total is None else total + term
    total = total[:scen] + total[scen:]
    for i in range(lines):
        outs[i][...] = total[i * rows : (i + 1) * rows]


def spread(index, grads, factors, lines):
    group = len(grads)
    scen, block = grads[0].shape
    line_rows, buses = factors.shape
    tile = tile_of(buses, 256)
    rows = scen // lines
    return pl.pallas_call(
        functools.partial(spread_kernel, group, lines),
        grid=(buses // tile,),
        in_specs=[pl.BlockSpec(memory_space=pltpu.SMEM)]
        + [pl.BlockSpec((scen, block), lambda i: (0, 0))] * group
        + [pl.BlockSpec((line_rows, tile), lambda i: (0, i))],
        out_specs=[pl.BlockSpec((rows, tile), lambda i: (0, i))] * lines,
        out_shape=[jax.ShapeDtypeStruct((rows, buses), F32)] * lines,
        scratch_shapes=[pltpu.VMEM((group, 2 * scen, block), F32)],
        cost_estimate=pl.CostEstimate(
            flops=8 * scen * buses * line_rows,
            bytes_accessed=4 * buses * line_rows,
            transcendentals=0,
        ),
        name="spread",
    )(index, *grads, factors)


def exchange(values, axis, size, stride, count):
    got = [values[0]]
    for j in range(1, count):
        pairs = [(d, d ^ (j * stride)) for d in range(size)]
        got.append(lax.ppermute(values[j], axis, pairs))
    return got


def body(lines, buses, injections, factors, outage_factors, outage_line, table, tier):
    scen = injections.shape[0]
    line_rows = factors.shape[0]
    outages = outage_factors.shape[1]
    group = min(4, buses)
    depth = buses // group
    block = line_rows // group
    bus = lax.axis_index("bus")
    line = lax.axis_index("line")
    local = jnp.stack([bus % group, line * line_rows]).astype(jnp.int32)
    outage_row = outage_line.reshape(1, outages)
    smem = pl.BlockSpec(memory_space=pltpu.SMEM)
    vmem = pl.BlockSpec(memory_space=pltpu.VMEM)

    def reduce_all(pieces):
        mine = tree_sum(exchange(pieces, "bus", buses, 1, group))
        return tree_sum(exchange([mine] * depth, "bus", buses, group, depth))

    def gather_all(mine):
        return exchange([mine] * group, "bus", buses, 1, group)

    pieces = partial_flows(injections, factors, group, local)
    flows = gather_all(reduce_all(pieces))
    picked = pl.pallas_call(
        functools.partial(pick_kernel, group),
        in_specs=[smem] + [vmem] * (group + 1),
        out_specs=vmem,
        out_shape=jax.ShapeDtypeStruct((scen, outages), F32),
        name="pick",
    )(local, outage_row, *flows)
    picked = exchange([picked] * lines, "line", lines, 1, lines)
    results = pl.pallas_call(
        functools.partial(outage_kernel, group, lines),
        in_specs=[smem, smem] + [vmem] * (group + lines + 2),
        out_specs=[vmem] * (group + 1),
        out_shape=[jax.ShapeDtypeStruct((scen, block), F32)] * group
        + [jax.ShapeDtypeStruct((scen + 8, outages), F32)],
        scratch_shapes=[
            pltpu.VMEM((group, outages, block), F32),
            pltpu.VMEM((group, table.shape[0], block), F32),
            pltpu.VMEM((2, outages, 128), F32),
            pltpu.VMEM((2, outages, 128), F32),
            pltpu.VMEM((group, scen, 8, block), F32),
            pltpu.VMEM((scen, 8, outages), F32),
            pltpu.VMEM((scen, 8, 128), F32),
        ],
        name="outage_stage",
    )(local, tier, *flows, *picked, outage_factors, table)
    direct, back = results[:group], results[group]
    backs = exchange([back] * lines, "line", lines, 1, lines)
    pieces = pl.pallas_call(
        functools.partial(carry_kernel, group, lines, 2.0 / (outages * buses)),
        in_specs=[smem] + [vmem] * (group + lines + 1),
        out_specs=[vmem] * group,
        out_shape=[jax.ShapeDtypeStruct((scen + 8, block), F32)] * group,
        name="carry",
    )(local, outage_row, *direct, *backs)
    total = reduce_all(pieces)
    mean_penalty = total[scen, :scen] / (line_rows * lines * outages * buses)
    grads = gather_all(total[:scen])
    order = jnp.stack([bus % group, line]).astype(jnp.int32)
    parts = spread(order, grads, factors, lines)
    injection_grad = tree_sum(exchange(parts, "line", lines, 1, lines))
    return injection_grad, mean_penalty


def solution(mesh):
    return jax.shard_map(
        functools.partial(body, mesh.shape["line"], mesh.shape["bus"]),
        mesh=mesh,
        in_specs=(
            P(None, "bus"),
            P("line", "bus"),
            P("line", "bus"),
            P("bus"),
            P(None, "line"),
            P(),
        ),
        out_specs=(P("line", "bus"), P()),
        check_vma=False,
    )
```

```python
import functools

import jax
import jax.numpy as jnp
from jax import lax
from jax.experimental import pallas as pl
from jax.experimental.pallas import tpu as pltpu
from jax.sharding import PartitionSpec as P


UNROLL = 64
F32 = jnp.float32
BF16 = jnp.bfloat16
NT = (((1,), (1,)), ((), ()))
NN = (((1,), (0,)), ((), ()))


def split(x, parts):
    pieces = []
    for _ in range(parts):
        piece = x.astype(BF16)
        pieces.append(piece)
        x = x - piece.astype(F32)
    return pieces


def tile_of(extent, most):
    best = extent
    for size in range(128, most + 1, 128):
        if extent % size == 0:
            best = size
    return best


def tree_sum(values):
    values = list(values)
    while len(values) > 1:
        values = [values[i] + values[i + 1] for i in range(0, len(values), 2)]
    return values[0]


def flow_kernel(group, tiles, index, inj_ref, factor_ref, *rest):
    outs, stacked = rest[:group], rest[group]
    scen = inj_ref.shape[0]
    step = pl.program_id(0)

    @pl.when(step == 0)
    def _():
        high, low = split(inj_ref[...], 2)
        stacked[:scen, :] = high
        stacked[scen:, :] = low

    high, low = split(factor_ref[...], 2)
    both = lax.dot_general(stacked[...], high, NT, preferred_element_type=F32)
    both += lax.dot_general(stacked[...], low, NT, preferred_element_type=F32)
    result = both[:scen] + both[scen:]
    width = result.shape[1]
    for j in range(group):
        for t in range(tiles):

            @pl.when(step == j * tiles + t)
            def _():
                outs[j][:, t * width : (t + 1) * width] = result


def partial_flows(injections, factors, group, index):
    scen, buses = injections.shape
    rows = factors.shape[0]
    block = rows // group
    tile = tile_of(block, 256)
    tiles = block // tile
    grid_spec = pltpu.PrefetchScalarGridSpec(
        num_scalar_prefetch=1,
        grid=(group * tiles,),
        in_specs=[
            pl.BlockSpec((scen, buses), lambda i, index: (0, 0)),
            pl.BlockSpec(
                (tile, buses),
                lambda i, index: ((index[0] ^ (i // tiles)) * tiles + i % tiles, 0),
            ),
        ],
        out_specs=[pl.BlockSpec((scen, block), lambda i, index: (0, 0))] * group,
        scratch_shapes=[pltpu.VMEM((2 * scen, buses), BF16)],
    )
    return pl.pallas_call(
        functools.partial(flow_kernel, group, tiles),
        grid_spec=grid_spec,
        out_shape=[jax.ShapeDtypeStruct((scen, block), F32)] * group,
        cost_estimate=pl.CostEstimate(
            flops=8 * scen * buses * rows,
            bytes_accessed=4 * buses * rows,
            transcendentals=0,
        ),
        name="partial_flows",
    )(index, injections, factors)


def chosen(index_ref, j, block, outage_row):
    rows = lax.broadcasted_iota(jnp.int32, (block, outage_row.shape[1]), 0)
    start = index_ref[1] + (index_ref[0] ^ j) * block
    return jnp.where(rows + start == outage_row, 1.0, 0.0).astype(BF16)


def pick_kernel(group, index_ref, line_ref, *rest):
    flows, out = rest[:group], rest[group]
    scen, block = flows[0].shape
    total = None
    for j in range(group):
        lhs = jnp.concatenate(split(flows[j][...], 3), axis=0)
        part = lax.dot_general(
            lhs,
            chosen(index_ref, j, block, line_ref[...]),
            NN,
            preferred_element_type=F32,
        )
        part = part[:scen] + part[scen : 2 * scen] + part[2 * scen :]
        total = part if total is None else total + part
    out[...] = total


def carry_kernel(group, backs, scale, index_ref, line_ref, *rest):
    direct = rest[:group]
    parts = rest[group : group + backs]
    outs = rest[group + backs :]
    scen, block = direct[0].shape
    back = tree_sum([part[...] for part in parts])
    lhs = jnp.concatenate(split(back[:scen], 3), axis=0)
    for j in range(group):
        part = lax.dot_general(
            lhs,
            chosen(index_ref, j, block, line_ref[...]),
            NT,
            preferred_element_type=F32,
        )
        part = part[:scen] + part[scen : 2 * scen] + part[2 * scen :]
        outs[j][:scen, :] = scale * (direct[j][...] + part)
        outs[j][scen:, :] = back[scen:, :block]


def outage_kernel(group, others, index_ref, tier_ref, *rest):
    flows = rest[:group]
    picked = rest[group : group + others]
    factor_ref, table_ref, tiers_ref = rest[group + others : group + others + 3]
    rest = rest[group + others + 3 :]
    direct = rest[:group]
    back_ref = rest[group]
    turned, level, all_picked, energy, wide, sums, held, held_back, pen, rows_pen = rest[
        group + 1 :
    ]
    scen, block = flows[0].shape
    outages = factor_ref.shape[1]
    lanes = 128
    cols = block // lanes
    both = 2

    all_picked[...] = tree_sum([ref[...] for ref in picked])
    for k in range(outages // lanes):
        cut = slice(k * lanes, (k + 1) * lanes)
        squares = None
        for j in range(group):
            start = pl.multiple_of((index_ref[0] ^ j) * block, lanes)
            for c in range(cols):
                part = factor_ref[pl.ds(start + c * lanes, lanes), cut].T
                turned[j, cut, c * lanes : (c + 1) * lanes] = part
                squares = part * part if squares is None else squares + part * part
        energy[cut, :] = squares
    for j in range(group):
        start = pl.multiple_of((index_ref[0] ^ j) * block, lanes)
        level[j] = 0.4 * table_ref[:, pl.ds(start, block)].astype(F32)

    def pair(step, carry):
        for r in range(both):
            row = all_picked[pl.ds(step * both + r, 1), :]
            for k in range(outages // lanes):
                part = row[:, k * lanes : (k + 1) * lanes]
                wide[r, k * lanes : (k + 1) * lanes, :] = jnp.broadcast_to(
                    part, (lanes, lanes)
                ).T
        losses = [None] * both
        for j in range(group):
            lows, highs, limits = [], [], []
            for r in range(both):
                s = step * both + r
                limit = level[j, pl.ds(tier_ref[s], 1), :]
                flow = flows[j][pl.ds(s, 1), :]
                low, high = -limit - flow, limit - flow
                for c in range(cols):
                    cut = slice(c * lanes, (c + 1) * lanes)
                    lows.append(jnp.broadcast_to(low[:, cut], (8, lanes)))
                    highs.append(jnp.broadcast_to(high[:, cut], (8, lanes)))
                    limits.append(limit[:, cut])

            def body(k, state):
                state = list(state)
                at = pl.ds(pl.multiple_of(k * 8, 8), 8)
                factors = [
                    turned[j, at, c * lanes : (c + 1) * lanes] for c in range(cols)
                ]
                for r in range(both):
                    flow = wide[r, at, :]
                    total = flow * energy[at, :] if j == 0 else sums[r, at, :]
                    for c in range(cols):
                        n = r * cols + c
                        raised = jnp.maximum(factors[c] * flow, lows[n])
                        inside = jnp.minimum(raised, highs[n])
                        state[2 * n] = state[2 * n] + raised
                        state[2 * n + 1] = state[2 * n + 1] + inside
                        total = total - inside * factors[c]
                    sums[r, at, :] = total
                return tuple(state)

            init = tuple([jnp.zeros((8, lanes), F32)] * (2 * both * cols))
            state = lax.fori_loop(0, outages // 8, body, init, unroll=UNROLL)
            for r in range(both):
                at = pl.ds(pl.multiple_of((step * both + r) * 8, 8), 8)
                for c in range(cols):
                    n = r * cols + c
                    raised, inside = state[2 * n], state[2 * n + 1]
                    held[j * cols + c, at, :] = inside
                    loss = limits[n] * (2.0 * raised - inside)
                    losses[r] = loss if losses[r] is None else losses[r] + loss
        for r in range(both):
            at = pl.ds(pl.multiple_of((step * both + r) * 8, 8), 8)
            pen[0, at, :] = losses[r]
            for k in range(outages // lanes):
                cut = slice(k * lanes, (k + 1) * lanes)
                held_back[k, at, :] = jnp.sum(
                    sums[r, cut, :].T.reshape(lanes // 8, 8, lanes), axis=0
                )
        return carry

    lax.fori_loop(0, scen // both, pair, 0)

    for j in range(group):
        direct[j][...] = jnp.dot(
            all_picked[...],
            turned[j],
            precision=lax.Precision.HIGHEST,
            preferred_element_type=F32,
        )

    def gathered(ref, step, first, count):
        whole = [
            tree_sum([ref[i, pl.ds(step * 64 + r, 8, stride=8), :] for r in range(8)])
            for i in range(first, first + count)
        ]
        return jnp.concatenate(whole, axis=1)

    def finish(step, carry):
        at = pl.ds(pl.multiple_of(step * 8, 8), 8)
        back = gathered(held_back, step, 0, outages // lanes)
        back_ref[at, :] = back
        gain = jnp.sum(all_picked[at, :] * back, axis=1, keepdims=True)
        tiers = tiers_ref[at, :]
        for j in range(group):
            every = direct[j][at, :]
            here = every - gathered(held, step, j * cols, cols)
            limit = jnp.zeros_like(here)
            for t in range(table_ref.shape[0]):
                limit = jnp.where(tiers == t, level[j, t : t + 1, :], limit)
            direct[j][at, :] = here
            gain += jnp.sum(
                flows[j][at, :] * here + limit * every, axis=1, keepdims=True
            )
        loss = jnp.sum(gathered(pen, step, 0, 1), axis=1, keepdims=True)
        rows_pen[at, :] = jnp.broadcast_to(gain - loss, (8, lanes))
        return carry

    lax.fori_loop(0, scen // 8, finish, 0)
    back_ref[scen:, :] = jnp.zeros((back_ref.shape[0] - scen, outages), F32)
    back_ref[scen : scen + 1, :scen] = rows_pen[...].T[:1, :]


def spread_kernel(group, lines, index_ref, *rest):
    grads = rest[:group]
    factor_ref = rest[group]
    outs = rest[group + 1 : group + 1 + lines]
    stacked = rest[group + 1 + lines]
    scen, block = grads[0].shape
    rows = scen // lines

    @pl.when(pl.program_id(0) == 0)
    def _():
        for j in range(group):
            for i in range(lines):
                at = pl.ds(pl.multiple_of((index_ref[1] ^ i) * rows, 8), rows)
                high, low = split(grads[j][at, :], 2)
                stacked[j, i * rows : (i + 1) * rows, :] = high.astype(F32)
                stacked[j, scen + i * rows : scen + (i + 1) * rows, :] = low.astype(F32)

    total = None
    for j in range(group):
        at = pl.ds(pl.multiple_of((index_ref[0] ^ j) * block, 8), block)
        lhs = stacked[j].astype(BF16)
        for part in split(factor_ref[at, :], 2):
            term = lax.dot_general(lhs, part, NN, preferred_element_type=F32)
            total = term if total is None else total + term
    total = total[:scen] + total[scen:]
    for i in range(lines):
        outs[i][...] = total[i * rows : (i + 1) * rows]


def spread(index, grads, factors, lines):
    group = len(grads)
    scen, block = grads[0].shape
    line_rows, buses = factors.shape
    tile = tile_of(buses, 256)
    rows = scen // lines
    return pl.pallas_call(
        functools.partial(spread_kernel, group, lines),
        grid=(buses // tile,),
        in_specs=[pl.BlockSpec(memory_space=pltpu.SMEM)]
        + [pl.BlockSpec((scen, block), lambda i: (0, 0))] * group
        + [pl.BlockSpec((line_rows, tile), lambda i: (0, i))],
        out_specs=[pl.BlockSpec((rows, tile), lambda i: (0, i))] * lines,
        out_shape=[jax.ShapeDtypeStruct((rows, buses), F32)] * lines,
        scratch_shapes=[pltpu.VMEM((group, 2 * scen, block), F32)],
        cost_estimate=pl.CostEstimate(
            flops=8 * scen * buses * line_rows,
            bytes_accessed=4 * buses * line_rows,
            transcendentals=0,
        ),
        name="spread",
    )(index, *grads, factors)


def exchange(values, axis, size, stride, count):
    got = [values[0]]
    for j in range(1, count):
        pairs = [(d, d ^ (j * stride)) for d in range(size)]
        got.append(lax.ppermute(values[j], axis, pairs))
    return got


def body(lines, buses, injections, factors, outage_factors, outage_line, table, tier):
    scen = injections.shape[0]
    line_rows = factors.shape[0]
    outages = outage_factors.shape[1]
    group = min(4, buses)
    depth = buses // group
    block = line_rows // group
    bus = lax.axis_index("bus")
    line = lax.axis_index("line")
    local = jnp.stack([bus % group, line * line_rows]).astype(jnp.int32)
    outage_row = outage_line.reshape(1, outages)
    smem = pl.BlockSpec(memory_space=pltpu.SMEM)
    vmem = pl.BlockSpec(memory_space=pltpu.VMEM)

    def reduce_all(pieces):
        mine = tree_sum(exchange(pieces, "bus", buses, 1, group))
        return tree_sum(exchange([mine] * depth, "bus", buses, group, depth))

    def gather_all(mine):
        return exchange([mine] * group, "bus", buses, 1, group)

    pieces = partial_flows(injections, factors, group, local)
    flows = gather_all(reduce_all(pieces))
    picked = pl.pallas_call(
        functools.partial(pick_kernel, group),
        in_specs=[smem] + [vmem] * (group + 1),
        out_specs=vmem,
        out_shape=jax.ShapeDtypeStruct((scen, outages), F32),
        name="pick",
    )(local, outage_row, *flows)
    picked = exchange([picked] * lines, "line", lines, 1, lines)
    results = pl.pallas_call(
        functools.partial(outage_kernel, group, lines),
        in_specs=[smem, smem] + [vmem] * (group + lines + 3),
        out_specs=[vmem] * (group + 1),
        out_shape=[jax.ShapeDtypeStruct((scen, block), F32)] * group
        + [jax.ShapeDtypeStruct((scen + 8, outages), F32)],
        scratch_shapes=[
            pltpu.VMEM((group, outages, block), F32),
            pltpu.VMEM((group, table.shape[0], block), F32),
            pltpu.VMEM((scen, outages), F32),
            pltpu.VMEM((outages, 128), F32),
            pltpu.VMEM((2, outages, 128), F32),
            pltpu.VMEM((2, outages, 128), F32),
            pltpu.VMEM((line_rows // 128, scen * 8, 128), F32),
            pltpu.VMEM((outages // 128, scen * 8, 128), F32),
            pltpu.VMEM((1, scen * 8, 128), F32),
            pltpu.VMEM((scen, 128), F32),
        ],
        name="outage_stage",
    )(local, tier, *flows, *picked, outage_factors, table, tier.reshape(scen, 1))
    direct, back = results[:group], results[group]
    backs = exchange([back] * lines, "line", lines, 1, lines)
    pieces = pl.pallas_call(
        functools.partial(carry_kernel, group, lines, 2.0 / (outages * buses)),
        in_specs=[smem] + [vmem] * (group + lines + 1),
        out_specs=[vmem] * group,
        out_shape=[jax.ShapeDtypeStruct((scen + 8, block), F32)] * group,
        name="carry",
    )(local, outage_row, *direct, *backs)
    total = reduce_all(pieces)
    mean_penalty = total[scen, :scen] / (line_rows * lines * outages * buses)
    grads = gather_all(total[:scen])
    order = jnp.stack([bus % group, line]).astype(jnp.int32)
    parts = spread(order, grads, factors, lines)
    injection_grad = tree_sum(exchange(parts, "line", lines, 1, lines))
    return injection_grad, mean_penalty


def solution(mesh):
    return jax.shard_map(
        functools.partial(body, mesh.shape["line"], mesh.shape["bus"]),
        mesh=mesh,
        in_specs=(
            P(None, "bus"),
            P("line", "bus"),
            P("line", "bus"),
            P("bus"),
            P(None, "line"),
            P(),
        ),
        out_specs=(P("line", "bus"), P()),
        check_vma=False,
    )
```

```python
import functools

import jax
import jax.numpy as jnp
from jax import lax
from jax.experimental import pallas as pl
from jax.experimental.pallas import tpu as pltpu
from jax.sharding import PartitionSpec as P


F32 = jnp.float32
BF16 = jnp.bfloat16
NT = (((1,), (1,)), ((), ()))
NN = (((1,), (0,)), ((), ()))


def split(x, parts):
    pieces = []
    for _ in range(parts):
        piece = x.astype(BF16)
        pieces.append(piece)
        x = x - piece.astype(F32)
    return pieces


def tile_of(extent, most):
    best = extent
    for size in range(128, most + 1, 128):
        if extent % size == 0:
            best = size
    return best


def tree_sum(values):
    values = list(values)
    while len(values) > 1:
        values = [values[i] + values[i + 1] for i in range(0, len(values), 2)]
    return values[0]


def flow_kernel(group, index_ref, inj_ref, factor_ref, *rest):
    outs = rest[:group]
    stacked, landed, arrived = rest[group:]
    scen = inj_ref.shape[0]
    count, tile, _ = landed.shape
    tiles = count // group

    def fetch(j, t):
        row = pl.multiple_of(((index_ref[0] ^ j) * tiles + t) * tile, 8)
        at = j * tiles + t
        return pltpu.make_async_copy(
            factor_ref.at[pl.ds(row, tile), :], landed.at[at], arrived.at[at]
        )

    for j in range(group):
        for t in range(tiles):
            fetch(j, t).start()
    high, low = split(inj_ref[...], 2)
    stacked[:scen, :] = high
    stacked[scen:, :] = low
    for j in range(group):

        def block(t, carry):
            fetch(j, t).wait()
            total = None
            for part in split(landed[j * tiles + t], 2):
                term = lax.dot_general(
                    part, stacked[...], NT, preferred_element_type=F32
                )
                total = term if total is None else total + term
            total = total.T
            at = pl.ds(pl.multiple_of(t * tile, tile), tile)
            outs[j][:, at] = total[:scen] + total[scen:]
            return carry

        lax.fori_loop(0, tiles, block, 0)


def partial_flows(injections, factors, group, index):
    scen, buses = injections.shape
    rows = factors.shape[0]
    block = rows // group
    tile = tile_of(block, 256)
    count = rows // tile
    vmem = pl.BlockSpec(memory_space=pltpu.VMEM)
    return pl.pallas_call(
        functools.partial(flow_kernel, group),
        in_specs=[
            pl.BlockSpec(memory_space=pltpu.SMEM),
            vmem,
            pl.BlockSpec(memory_space=pl.ANY),
        ],
        out_specs=[vmem] * group,
        out_shape=[jax.ShapeDtypeStruct((scen, block), F32)] * group,
        scratch_shapes=[
            pltpu.VMEM((2 * scen, buses), BF16),
            pltpu.VMEM((count, tile, buses), F32),
            pltpu.SemaphoreType.DMA((count,)),
        ],
        cost_estimate=pl.CostEstimate(
            flops=8 * scen * buses * rows,
            bytes_accessed=4 * buses * rows,
            transcendentals=0,
        ),
        name="partial_flows",
        compiler_params=pltpu.CompilerParams(vmem_limit_bytes=50 << 20),
    )(index, injections, factors)


def chosen(index_ref, j, block, outage_row):
    rows = lax.broadcasted_iota(jnp.int32, (block, outage_row.shape[1]), 0)
    start = index_ref[1] + (index_ref[0] ^ j) * block
    return jnp.where(rows + start == outage_row, 1.0, 0.0).astype(BF16)


def pick_kernel(group, index_ref, line_ref, *rest):
    flows, out = rest[:group], rest[group]
    scen, block = flows[0].shape
    total = None
    for j in range(group):
        lhs = jnp.concatenate(split(flows[j][...], 3), axis=0)
        part = lax.dot_general(
            lhs,
            chosen(index_ref, j, block, line_ref[...]),
            NN,
            preferred_element_type=F32,
        )
        part = part[:scen] + part[scen : 2 * scen] + part[2 * scen :]
        total = part if total is None else total + part
    out[...] = total


def carry_kernel(group, backs, scale, index_ref, line_ref, *rest):
    direct = rest[:group]
    parts = rest[group : group + backs]
    outs = rest[group + backs :]
    scen, block = direct[0].shape
    back = tree_sum([part[...] for part in parts])
    lhs = jnp.concatenate(split(back[:scen], 3), axis=0)
    for j in range(group):
        part = lax.dot_general(
            lhs,
            chosen(index_ref, j, block, line_ref[...]),
            NT,
            preferred_element_type=F32,
        )
        part = part[:scen] + part[scen : 2 * scen] + part[2 * scen :]
        outs[j][:scen, :] = scale * (direct[j][...] + part)
        outs[j][scen:, :] = back[scen:, :block]


def outage_kernel(group, others, index_ref, tier_ref, *rest):
    flows = rest[:group]
    picked = rest[group : group + others]
    factor_ref, table_ref, tiers_ref = rest[group + others : group + others + 3]
    rest = rest[group + others + 3 :]
    direct = rest[:group]
    back_ref = rest[group]
    turned, level, all_picked, rows, energy, wide, sums, held, held_back, pen, rows_pen = rest[
        group + 1 :
    ]
    scen, block = flows[0].shape
    outages = factor_ref.shape[1]
    lanes = 128
    cols = block // lanes
    both = 2

    all_picked[...] = tree_sum([ref[...] for ref in picked])
    for k in range(outages // lanes):
        cut = slice(k * lanes, (k + 1) * lanes)
        squares = None
        for j in range(group):
            start = pl.multiple_of((index_ref[0] ^ j) * block, lanes)
            for c in range(cols):
                part = factor_ref[pl.ds(start + c * lanes, lanes), cut].T
                turned[j, cut, c * lanes : (c + 1) * lanes] = part
                squares = part * part if squares is None else squares + part * part
        energy[cut, :] = squares
    for j in range(group):
        start = pl.multiple_of((index_ref[0] ^ j) * block, lanes)
        level[j] = 0.4 * table_ref[:, pl.ds(start, block)].astype(F32)

    tiles = outages // lanes

    for k in range(tiles):
        rows[k] = all_picked[:, k * lanes : (k + 1) * lanes]

    def widen(r, s, k):
        at = pl.ds(pl.multiple_of(k * lanes, lanes), lanes)
        row = rows[k, pl.ds(s, 1), :]
        wide[r, at, :] = jnp.broadcast_to(row, (lanes, lanes)).T

    def fold(r, place, k):
        at = pl.ds(pl.multiple_of(k * lanes, lanes), lanes)
        to = pl.ds(pl.multiple_of(place * 8, 8), 8)
        turned_sums = sums[r, at, :].T
        held_back[k, to, :] = tree_sum(
            [turned_sums[8 * i : 8 * (i + 1)] for i in range(lanes // 8)]
        )

    def pair(step, carry):
        losses = [None] * both
        for j in range(group):
            lows, highs, limits = [], [], []
            for r in range(both):
                s = step * both + r
                limit = level[j, pl.ds(tier_ref[s], 1), :]
                flow = flows[j][pl.ds(s, 1), :]
                low, high = -limit - flow, limit - flow
                for c in range(cols):
                    cut = slice(c * lanes, (c + 1) * lanes)
                    lows.append(jnp.broadcast_to(low[:, cut], (8, lanes)))
                    highs.append(jnp.broadcast_to(high[:, cut], (8, lanes)))
                    limits.append(limit[:, cut])

            def body(tile, state):
                state = list(state)
                if j == 0:
                    for r in range(both):
                        fold(r, step * both + r, tile)
                for k in range(lanes // 8):
                    at = pl.ds(pl.multiple_of(tile * lanes + k * 8, 8), 8)
                    factors = [
                        turned[j, at, c * lanes : (c + 1) * lanes] for c in range(cols)
                    ]
                    for r in range(both):
                        flow = wide[r, at, :]
                        total = flow * energy[at, :] if j == 0 else sums[r, at, :]
                        for c in range(cols):
                            n = r * cols + c
                            raised = jnp.maximum(factors[c] * flow, lows[n])
                            inside = jnp.minimum(raised, highs[n])
                            state[2 * n] = state[2 * n] + raised
                            state[2 * n + 1] = state[2 * n + 1] + inside
                            total = total - inside * factors[c]
                        sums[r, at, :] = total
                if j == group - 1:
                    later = jnp.minimum(step + 1, scen // both - 1)
                    for r in range(both):
                        widen(r, later * both + r, tile)
                return tuple(state)

            init = tuple([jnp.zeros((8, lanes), F32)] * (2 * both * cols))
            state = lax.fori_loop(0, tiles, body, init)
            for r in range(both):
                at = pl.ds(pl.multiple_of((step * both + r) * 8, 8), 8)
                for c in range(cols):
                    n = r * cols + c
                    raised, inside = state[2 * n], state[2 * n + 1]
                    held[j * cols + c, at, :] = inside
                    loss = limits[n] * (2.0 * raised - inside)
                    losses[r] = loss if losses[r] is None else losses[r] + loss
        for r in range(both):
            at = pl.ds(pl.multiple_of((step * both + r) * 8, 8), 8)
            pen[0, at, :] = losses[r]
        return carry

    sums[...] = jnp.zeros_like(sums)
    for r in range(both):
        for k in range(tiles):
            widen(r, r, k)
    lax.fori_loop(0, scen // both, pair, 0)
    for r in range(both):
        for k in range(tiles):
            fold(r, scen + r, k)

    for j in range(group):
        direct[j][...] = jnp.dot(
            all_picked[...],
            turned[j],
            precision=lax.Precision.HIGHEST,
            preferred_element_type=F32,
        )

    def gathered(ref, step, first, count, skip=0):
        base = (step * 8 + skip) * 8
        whole = [
            tree_sum([ref[i, pl.ds(base + r, 8, stride=8), :] for r in range(8)])
            for i in range(first, first + count)
        ]
        return jnp.concatenate(whole, axis=1)

    def finish(step, carry):
        at = pl.ds(pl.multiple_of(step * 8, 8), 8)
        back = gathered(held_back, step, 0, outages // lanes, both)
        back_ref[at, :] = back
        gain = jnp.sum(all_picked[at, :] * back, axis=1, keepdims=True)
        tiers = tiers_ref[at, :]
        for j in range(group):
            every = direct[j][at, :]
            here = every - gathered(held, step, j * cols, cols)
            limit = jnp.zeros_like(here)
            for t in range(table_ref.shape[0]):
                limit = jnp.where(tiers == t, level[j, t : t + 1, :], limit)
            direct[j][at, :] = here
            gain += jnp.sum(
                flows[j][at, :] * here + limit * every, axis=1, keepdims=True
            )
        loss = jnp.sum(gathered(pen, step, 0, 1), axis=1, keepdims=True)
        rows_pen[at, :] = jnp.broadcast_to(gain - loss, (8, lanes))
        return carry

    lax.fori_loop(0, scen // 8, finish, 0)
    back_ref[scen:, :] = jnp.zeros((back_ref.shape[0] - scen, outages), F32)
    back_ref[scen : scen + 1, :scen] = rows_pen[...].T[:1, :]


def spread_kernel(group, lines, index_ref, *rest):
    grads = rest[:group]
    factor_ref = rest[group]
    outs = rest[group + 1 : group + 1 + lines]
    stacked, landed, arrived = rest[group + 1 + lines :]
    scen, block = grads[0].shape
    rows = scen // lines
    count, _, tile = landed.shape

    def fetch(t):
        return pltpu.make_async_copy(
            factor_ref.at[:, pl.ds(pl.multiple_of(t * tile, tile), tile)],
            landed.at[t],
            arrived.at[t],
        )

    for t in range(count):
        fetch(t).start()
    for j in range(group):
        for i in range(lines):
            at = pl.ds(pl.multiple_of((index_ref[1] ^ i) * rows, 8), rows)
            high, low = split(grads[j][at, :], 2)
            stacked[j, i * rows : (i + 1) * rows, :] = high.astype(F32)
            stacked[j, scen + i * rows : scen + (i + 1) * rows, :] = low.astype(F32)

    def piece(t, carry):
        fetch(t).wait()
        total = None
        for j in range(group):
            at = pl.ds(pl.multiple_of((index_ref[0] ^ j) * block, 8), block)
            lhs = stacked[j].astype(BF16)
            for part in split(landed[t, at, :], 2):
                term = lax.dot_general(lhs, part, NN, preferred_element_type=F32)
                total = term if total is None else total + term
        total = total[:scen] + total[scen:]
        for i in range(lines):
            outs[i][:, pl.ds(pl.multiple_of(t * tile, tile), tile)] = total[
                i * rows : (i + 1) * rows
            ]
        return carry

    lax.fori_loop(0, count, piece, 0)


def spread(index, grads, factors, lines):
    group = len(grads)
    scen, block = grads[0].shape
    line_rows, buses = factors.shape
    tile = tile_of(buses, 256)
    count = buses // tile
    rows = scen // lines
    vmem = pl.BlockSpec(memory_space=pltpu.VMEM)
    return pl.pallas_call(
        functools.partial(spread_kernel, group, lines),
        in_specs=[pl.BlockSpec(memory_space=pltpu.SMEM)]
        + [vmem] * group
        + [pl.BlockSpec(memory_space=pl.ANY)],
        out_specs=[vmem] * lines,
        out_shape=[jax.ShapeDtypeStruct((rows, buses), F32)] * lines,
        scratch_shapes=[
            pltpu.VMEM((group, 2 * scen, block), F32),
            pltpu.VMEM((count, line_rows, tile), F32),
            pltpu.SemaphoreType.DMA((count,)),
        ],
        cost_estimate=pl.CostEstimate(
            flops=8 * scen * buses * line_rows,
            bytes_accessed=4 * buses * line_rows,
            transcendentals=0,
        ),
        name="spread",
        compiler_params=pltpu.CompilerParams(vmem_limit_bytes=42 << 20),
    )(index, *grads, factors)


def exchange(values, axis, size, stride, count):
    got = [values[0]]
    for j in range(1, count):
        pairs = [(d, d ^ (j * stride)) for d in range(size)]
        got.append(lax.ppermute(values[j], axis, pairs))
    return got


def body(lines, buses, injections, factors, outage_factors, outage_line, table, tier):
    scen = injections.shape[0]
    line_rows = factors.shape[0]
    outages = outage_factors.shape[1]
    group = min(4, buses)
    depth = buses // group
    block = line_rows // group
    bus = lax.axis_index("bus")
    line = lax.axis_index("line")
    local = jnp.stack([bus % group, line * line_rows]).astype(jnp.int32)
    outage_row = outage_line.reshape(1, outages)
    smem = pl.BlockSpec(memory_space=pltpu.SMEM)
    vmem = pl.BlockSpec(memory_space=pltpu.VMEM)

    def reduce_all(pieces):
        mine = tree_sum(exchange(pieces, "bus", buses, 1, group))
        return tree_sum(exchange([mine] * depth, "bus", buses, group, depth))

    def gather_all(mine):
        return exchange([mine] * group, "bus", buses, 1, group)

    pieces = partial_flows(injections, factors, group, local)
    flows = gather_all(reduce_all(pieces))
    picked = pl.pallas_call(
        functools.partial(pick_kernel, group),
        in_specs=[smem] + [vmem] * (group + 1),
        out_specs=vmem,
        out_shape=jax.ShapeDtypeStruct((scen, outages), F32),
        name="pick",
        compiler_params=pltpu.CompilerParams(vmem_limit_bytes=8 << 20),
    )(local, outage_row, *flows)
    picked = exchange([picked] * lines, "line", lines, 1, lines)
    results = pl.pallas_call(
        functools.partial(outage_kernel, group, lines),
        in_specs=[smem, smem] + [vmem] * (group + lines + 3),
        out_specs=[vmem] * (group + 1),
        out_shape=[jax.ShapeDtypeStruct((scen, block), F32)] * group
        + [jax.ShapeDtypeStruct((scen + 8, outages), F32)],
        scratch_shapes=[
            pltpu.VMEM((group, outages, block), F32),
            pltpu.VMEM((group, table.shape[0], block), F32),
            pltpu.VMEM((scen, outages), F32),
            pltpu.VMEM((outages // 128, scen, 128), F32),
            pltpu.VMEM((outages, 128), F32),
            pltpu.VMEM((2, outages, 128), F32),
            pltpu.VMEM((2, outages, 128), F32),
            pltpu.VMEM((line_rows // 128, scen * 8, 128), F32),
            pltpu.VMEM((outages // 128, (scen + 2) * 8, 128), F32),
            pltpu.VMEM((1, scen * 8, 128), F32),
            pltpu.VMEM((scen, 128), F32),
        ],
        name="outage_stage",
        compiler_params=pltpu.CompilerParams(vmem_limit_bytes=24 << 20),
    )(local, tier, *flows, *picked, outage_factors, table, tier.reshape(scen, 1))
    direct, back = results[:group], results[group]
    backs = exchange([back] * lines, "line", lines, 1, lines)
    pieces = pl.pallas_call(
        functools.partial(carry_kernel, group, lines, 2.0 / (outages * buses)),
        in_specs=[smem] + [vmem] * (group + lines + 1),
        out_specs=[vmem] * group,
        out_shape=[jax.ShapeDtypeStruct((scen + 8, block), F32)] * group,
        name="carry",
        compiler_params=pltpu.CompilerParams(vmem_limit_bytes=8 << 20),
    )(local, outage_row, *direct, *backs)
    total = reduce_all(pieces)
    mean_penalty = total[scen, :scen] / (line_rows * lines * outages * buses)
    grads = gather_all(total[:scen])
    order = jnp.stack([bus % group, line]).astype(jnp.int32)
    parts = spread(order, grads, factors, lines)
    injection_grad = tree_sum(exchange(parts, "line", lines, 1, lines))
    return injection_grad, mean_penalty


def solution(mesh):
    return jax.shard_map(
        functools.partial(body, mesh.shape["line"], mesh.shape["bus"]),
        mesh=mesh,
        in_specs=(
            P(None, "bus"),
            P("line", "bus"),
            P("line", "bus"),
            P("bus"),
            P(None, "line"),
            P(),
        ),
        out_specs=(P("line", "bus"), P()),
        check_vma=False,
    )
```

```python
import functools

import jax
import jax.numpy as jnp
from jax import lax
from jax.experimental import pallas as pl
from jax.experimental.pallas import tpu as pltpu
from jax.sharding import PartitionSpec as P


SEND_LIMIT = 40
F32 = jnp.float32
BF16 = jnp.bfloat16
NT = (((1,), (1,)), ((), ()))
NN = (((1,), (0,)), ((), ()))


def split(x, parts):
    pieces = []
    for _ in range(parts):
        piece = x.astype(BF16)
        pieces.append(piece)
        x = x - piece.astype(F32)
    return pieces


def tile_of(extent, most):
    best = extent
    for size in range(128, most + 1, 128):
        if extent % size == 0:
            best = size
    return best


def tree_sum(values):
    values = list(values)
    while len(values) > 1:
        values = [values[i] + values[i + 1] for i in range(0, len(values), 2)]
    return values[0]


def flow_kernel(digits, fresh, index_ref, inj_ref, factor_ref, *rest):
    outs = rest[: len(digits)]
    if fresh:
        stacked, landed, arrived = rest[len(digits) :]
    else:
        stacked = inj_ref
        landed, arrived = rest[len(digits) :]
    count, tile, _ = landed.shape
    tiles = count // len(digits)

    def fetch(i, t):
        row = ((index_ref[0] ^ digits[i]) * tiles + t) * tile
        at = i * tiles + t
        return pltpu.make_async_copy(
            factor_ref.at[pl.ds(pl.multiple_of(row, tile), tile), :],
            landed.at[at],
            arrived.at[at],
        )

    for i in range(len(digits)):
        for t in range(tiles):
            fetch(i, t).start()
    scen = stacked.shape[0] // 2
    if fresh:
        high, low = split(inj_ref[...], 2)
        stacked[:scen, :] = high
        stacked[scen:, :] = low
    for i in range(len(digits)):

        def block(t, carry):
            fetch(i, t).wait()
            total = None
            for part in split(landed[i * tiles + t], 2):
                term = lax.dot_general(
                    part, stacked[...], NT, preferred_element_type=F32
                )
                total = term if total is None else total + term
            total = total.T
            at = pl.ds(pl.multiple_of(t * tile, tile), tile)
            outs[i][:, at] = total[:scen] + total[scen:]
            return carry

        lax.fori_loop(0, tiles, block, 0)


def partial_flows(injections, factors, group, digits, fresh, index, limit):
    rows, buses = factors.shape
    scen = injections.shape[0] if fresh else injections.shape[0] // 2
    block = rows // group
    tile = tile_of(block, 256)
    count = len(digits) * (block // tile)
    vmem = pl.BlockSpec(memory_space=pltpu.VMEM)
    stacked = [jax.ShapeDtypeStruct((2 * scen, buses), BF16)] if fresh else []
    return pl.pallas_call(
        functools.partial(flow_kernel, digits, fresh),
        in_specs=[
            pl.BlockSpec(memory_space=pltpu.SMEM),
            vmem,
            pl.BlockSpec(memory_space=pl.ANY),
        ],
        out_specs=[vmem] * (len(digits) + fresh),
        out_shape=[jax.ShapeDtypeStruct((scen, block), F32)] * len(digits) + stacked,
        scratch_shapes=[
            pltpu.VMEM((count, tile, buses), F32),
            pltpu.SemaphoreType.DMA((count,)),
        ],
        cost_estimate=pl.CostEstimate(
            flops=8 * scen * buses * count * tile,
            bytes_accessed=4 * buses * count * tile,
            transcendentals=0,
        ),
        name="partial_flows",
        compiler_params=pltpu.CompilerParams(vmem_limit_bytes=limit << 20),
    )(index, injections, factors)


def chosen(index_ref, j, block, outage_row):
    rows = lax.broadcasted_iota(jnp.int32, (block, outage_row.shape[1]), 0)
    start = index_ref[1] + (index_ref[0] ^ j) * block
    return jnp.where(rows + start == outage_row, 1.0, 0.0).astype(BF16)


def pick_kernel(group, index_ref, line_ref, *rest):
    flows, out = rest[:group], rest[group]
    scen, block = flows[0].shape
    total = None
    for j in range(group):
        lhs = jnp.concatenate(split(flows[j][...], 3), axis=0)
        part = lax.dot_general(
            lhs,
            chosen(index_ref, j, block, line_ref[...]),
            NN,
            preferred_element_type=F32,
        )
        part = part[:scen] + part[scen : 2 * scen] + part[2 * scen :]
        total = part if total is None else total + part
    out[...] = total


def carry_kernel(group, backs, scale, index_ref, line_ref, *rest):
    direct = rest[:group]
    parts = rest[group : group + backs]
    outs = rest[group + backs :]
    scen, block = direct[0].shape
    back = tree_sum([part[...] for part in parts])
    lhs = jnp.concatenate(split(back[:scen], 3), axis=0)
    for j in range(group):
        part = lax.dot_general(
            lhs,
            chosen(index_ref, j, block, line_ref[...]),
            NT,
            preferred_element_type=F32,
        )
        part = part[:scen] + part[scen : 2 * scen] + part[2 * scen :]
        outs[j][:scen, :] = scale * (direct[j][...] + part)
        outs[j][scen:, :] = back[scen:, :block]


def turn_kernel(group, index_ref, factor_ref, turned, energy, landed, arrived):
    lanes = 128
    _, outages, block = turned.shape

    def fetch(j):
        start = pl.multiple_of((index_ref[0] ^ j) * block, lanes)
        return pltpu.make_async_copy(
            factor_ref.at[pl.ds(start, block), :], landed.at[j], arrived.at[j]
        )

    for j in range(group):
        fetch(j).start()
    for j in range(group):
        fetch(j).wait()
        for k in range(outages // lanes):
            cut = slice(k * lanes, (k + 1) * lanes)
            squares = jnp.zeros((lanes, lanes), F32) if j == 0 else energy[cut, :]
            for c in range(block // lanes):
                place = slice(c * lanes, (c + 1) * lanes)
                part = landed[j, place, cut].T
                turned[j, cut, place] = part
                squares = squares + part * part
            energy[cut, :] = squares


def outage_kernel(group, others, index_ref, tier_ref, *rest):
    flows = rest[:group]
    picked = rest[group : group + others]
    turned, energy, table_ref, tiers_ref = rest[group + others : group + others + 4]
    rest = rest[group + others + 4 :]
    direct = rest[:group]
    back_ref = rest[group]
    level, all_picked, rows, wide, sums, held, held_back, pen, rows_pen, tier_rows = rest[
        group + 1 :
    ]
    scen, block = flows[0].shape
    outages = energy.shape[0]
    lanes = 128
    cols = block // lanes
    both = 2

    all_picked[...] = tree_sum([ref[...] for ref in picked])
    for j in range(group):
        start = pl.multiple_of((index_ref[0] ^ j) * block, lanes)
        level[j] = 0.4 * table_ref[:, pl.ds(start, block)].astype(F32)

    tiles = outages // lanes

    for k in range(tiles):
        rows[k] = all_picked[:, k * lanes : (k + 1) * lanes]

    def widen(r, s, k):
        at = pl.ds(pl.multiple_of(k * lanes, lanes), lanes)
        row = rows[k, pl.ds(s, 1), :]
        wide[r, at, :] = jnp.broadcast_to(row, (lanes, lanes)).T

    def fold(r, place, k):
        at = pl.ds(pl.multiple_of(k * lanes, lanes), lanes)
        to = pl.ds(pl.multiple_of(place * 8, 8), 8)
        turned_sums = sums[r, at, :].T
        held_back[k, to, :] = tree_sum(
            [turned_sums[8 * i : 8 * (i + 1)] for i in range(lanes // 8)]
        )

    tier_rows[...] = jnp.broadcast_to(tiers_ref[...].astype(F32), (lanes, scen)).T

    def pair(step, carry):
        losses = [None] * both
        for j in range(group):
            lows, highs, limits = [], [], []
            for r in range(both):
                s = step * both + r
                limit = level[j, pl.ds(tier_ref[s], 1), :]
                flow = flows[j][pl.ds(s, 1), :]
                low, high = -limit - flow, limit - flow
                for c in range(cols):
                    cut = slice(c * lanes, (c + 1) * lanes)
                    lows.append(jnp.broadcast_to(low[:, cut], (8, lanes)))
                    highs.append(jnp.broadcast_to(high[:, cut], (8, lanes)))
                    limits.append(limit[:, cut])

            def body(tile, state):
                state = list(state)
                if j == 0:
                    for r in range(both):
                        fold(r, step * both + r, tile)
                for k in range(lanes // 8):
                    at = pl.ds(pl.multiple_of(tile * lanes + k * 8, 8), 8)
                    factors = [
                        turned[j, at, c * lanes : (c + 1) * lanes] for c in range(cols)
                    ]
                    for r in range(both):
                        flow = wide[r, at, :]
                        total = flow * energy[at, :] if j == 0 else sums[r, at, :]
                        for c in range(cols):
                            n = r * cols + c
                            raised = jnp.maximum(factors[c] * flow, lows[n])
                            inside = jnp.minimum(raised, highs[n])
                            state[2 * n] = state[2 * n] + raised
                            state[2 * n + 1] = state[2 * n + 1] + inside
                            total = total - inside * factors[c]
                        sums[r, at, :] = total
                if j == group - 1:
                    later = jnp.minimum(step + 1, scen // both - 1)
                    for r in range(both):
                        widen(r, later * both + r, tile)
                return tuple(state)

            init = tuple([jnp.zeros((8, lanes), F32)] * (2 * both * cols))
            state = lax.fori_loop(0, tiles, body, init)
            for r in range(both):
                at = pl.ds(pl.multiple_of((step * both + r) * 8, 8), 8)
                for c in range(cols):
                    n = r * cols + c
                    raised, inside = state[2 * n], state[2 * n + 1]
                    held[j * cols + c, at, :] = inside
                    loss = limits[n] * (2.0 * raised - inside)
                    losses[r] = loss if losses[r] is None else losses[r] + loss
        for r in range(both):
            at = pl.ds(pl.multiple_of((step * both + r) * 8, 8), 8)
            pen[0, at, :] = losses[r]
        return carry

    sums[...] = jnp.zeros_like(sums)
    for r in range(both):
        for k in range(tiles):
            widen(r, r, k)
    lax.fori_loop(0, scen // both, pair, 0)
    for r in range(both):
        for k in range(tiles):
            fold(r, scen + r, k)

    for j in range(group):
        direct[j][...] = jnp.dot(
            all_picked[...],
            turned[j],
            precision=lax.Precision.HIGHEST,
            preferred_element_type=F32,
        )

    def gathered(ref, step, first, count, skip=0):
        base = (step * 8 + skip) * 8
        whole = [
            tree_sum([ref[i, pl.ds(base + r, 8, stride=8), :] for r in range(8)])
            for i in range(first, first + count)
        ]
        return jnp.concatenate(whole, axis=1)

    def finish(step, carry):
        at = pl.ds(pl.multiple_of(step * 8, 8), 8)
        back = gathered(held_back, step, 0, outages // lanes, both)
        back_ref[at, :] = back
        gain = jnp.sum(all_picked[at, :] * back, axis=1, keepdims=True)
        tiers = tier_rows[at, :1]
        for j in range(group):
            every = direct[j][at, :]
            here = every - gathered(held, step, j * cols, cols)
            limit = jnp.zeros_like(here)
            for t in range(table_ref.shape[0]):
                limit = jnp.where(tiers == t, level[j, t : t + 1, :], limit)
            direct[j][at, :] = here
            gain += jnp.sum(
                flows[j][at, :] * here + limit * every, axis=1, keepdims=True
            )
        loss = jnp.sum(gathered(pen, step, 0, 1), axis=1, keepdims=True)
        rows_pen[at, :] = jnp.broadcast_to(gain - loss, (8, lanes))
        return carry

    lax.fori_loop(0, scen // 8, finish, 0)
    back_ref[scen:, :] = jnp.zeros((back_ref.shape[0] - scen, outages), F32)
    back_ref[scen : scen + 1, :scen] = rows_pen[...].T[:1, :]


def spread_kernel(digits, lines, more, index_ref, *rest):
    grads = rest[: len(digits)]
    factor_ref = rest[len(digits)]
    rest = rest[len(digits) + 1 :]
    if more:
        begun_ref, rest = rest[0], rest[1:]
    outs, (stacked, landed, arrived) = rest[:-3], rest[-3:]
    scen, block = grads[0].shape
    rows = scen // lines
    steps, _, tile = landed.shape

    def fetch(step, i):
        row = pl.multiple_of((index_ref[0] ^ digits[i]) * block, 8)
        cut = pl.ds(pl.multiple_of(step * tile, tile), tile)
        return pltpu.make_async_copy(
            factor_ref.at[pl.ds(row, block), cut],
            landed.at[step, pl.ds(i * block, block), :],
            arrived.at[step, i],
        )

    for step in range(steps):
        for i in range(len(digits)):
            fetch(step, i).start()
    for j in range(len(digits)):
        for i in range(lines):
            at = pl.ds(pl.multiple_of((index_ref[1] ^ i) * rows, 8), rows)
            high, low = split(grads[j][at, :], 2)
            stacked[j, i * rows : (i + 1) * rows, :] = high.astype(F32)
            stacked[j, scen + i * rows : scen + (i + 1) * rows, :] = low.astype(F32)

    def piece(step, carry):
        cut = pl.ds(pl.multiple_of(step * tile, tile), tile)
        total = None
        for j in range(len(digits)):
            fetch(step, j).wait()
        for j in range(len(digits)):
            lhs = stacked[j].astype(BF16)
            for part in split(landed[step, j * block : (j + 1) * block, :], 2):
                term = lax.dot_general(lhs, part, NN, preferred_element_type=F32)
                total = term if total is None else total + term
        total = total[:scen] + total[scen:]
        if more:
            total = total + begun_ref[:, cut]
        count = scen // len(outs)
        for i in range(len(outs)):
            outs[i][:, cut] = total[i * count : (i + 1) * count]
        return carry

    lax.fori_loop(0, steps, piece, 0)


def spread(index, grads, digits, begun, factors, lines, limit):
    scen, block = grads[0].shape
    buses = factors.shape[1]
    tile = tile_of(buses, 256)
    steps = buses // tile
    more = begun is not None
    outs = lines if more else 1
    vmem = pl.BlockSpec(memory_space=pltpu.VMEM)
    return pl.pallas_call(
        functools.partial(spread_kernel, digits, lines, more),
        in_specs=[pl.BlockSpec(memory_space=pltpu.SMEM)]
        + [vmem] * len(grads)
        + [pl.BlockSpec(memory_space=pl.ANY)]
        + [vmem] * more,
        out_specs=[vmem] * outs,
        out_shape=[jax.ShapeDtypeStruct((scen // outs, buses), F32)] * outs,
        scratch_shapes=[
            pltpu.VMEM((len(grads), 2 * scen, block), F32),
            pltpu.VMEM((steps, len(grads) * block, tile), F32),
            pltpu.SemaphoreType.DMA((steps, len(grads))),
        ],
        cost_estimate=pl.CostEstimate(
            flops=8 * scen * buses * block * len(grads),
            bytes_accessed=4 * buses * block * len(grads),
            transcendentals=0,
        ),
        name="spread",
        compiler_params=pltpu.CompilerParams(vmem_limit_bytes=limit << 20),
    )(index, *grads, factors, *([begun] if more else []))


def exchange(values, axis, size, stride, count):
    got = [values[0]]
    for j in range(1, count):
        pairs = [(d, d ^ (j * stride)) for d in range(size)]
        got.append(lax.ppermute(values[j], axis, pairs))
    return got


def body(lines, buses, *args):
    return staged(lines, buses, *args)


def staged(lines, buses, injections, factors, outage_factors, outage_line, table, tier):
    scen = injections.shape[0]
    line_rows = factors.shape[0]
    outages = outage_factors.shape[1]
    group = min(4, buses)
    depth = buses // group
    block = line_rows // group
    bus = lax.axis_index("bus")
    line = lax.axis_index("line")
    local = jnp.stack([bus % group, line * line_rows]).astype(jnp.int32)
    order = jnp.stack([bus % group, line]).astype(jnp.int32)
    outage_row = outage_line.reshape(1, outages)
    smem = pl.BlockSpec(memory_space=pltpu.SMEM)
    vmem = pl.BlockSpec(memory_space=pltpu.VMEM)
    away = tuple(range(1, group))

    def reduce_all(pieces):
        mine = tree_sum(exchange(pieces, "bus", buses, 1, group))
        return tree_sum(exchange([mine] * depth, "bus", buses, group, depth))

    def gather_all(mine):
        return exchange([mine] * group, "bus", buses, 1, group)

    *sent, stacked = partial_flows(
        injections, factors, group, away, True, local, SEND_LIMIT
    )
    own = partial_flows(stacked, factors, group, (0,), False, local, 40)
    flows = gather_all(reduce_all([*own, *sent]))
    turned, energy = pl.pallas_call(
        functools.partial(turn_kernel, group),
        in_specs=[smem, pl.BlockSpec(memory_space=pl.ANY)],
        out_specs=[vmem] * 2,
        out_shape=[
            jax.ShapeDtypeStruct((group, outages, block), F32),
            jax.ShapeDtypeStruct((outages, 128), F32),
        ],
        scratch_shapes=[
            pltpu.VMEM((group, block, outages), F32),
            pltpu.SemaphoreType.DMA((group,)),
        ],
        cost_estimate=pl.CostEstimate(
            flops=2 * line_rows * outages,
            bytes_accessed=12 * line_rows * outages,
            transcendentals=0,
        ),
        name="turn",
        compiler_params=pltpu.CompilerParams(vmem_limit_bytes=6 << 20),
    )(local, outage_factors)
    picked = pl.pallas_call(
        functools.partial(pick_kernel, group),
        in_specs=[smem] + [vmem] * (group + 1),
        out_specs=vmem,
        out_shape=jax.ShapeDtypeStruct((scen, outages), F32),
        name="pick",
        compiler_params=pltpu.CompilerParams(vmem_limit_bytes=5 << 20),
    )(local, outage_row, *flows)
    picked = exchange([picked] * lines, "line", lines, 1, lines)
    results = pl.pallas_call(
        functools.partial(outage_kernel, group, lines),
        in_specs=[smem, smem] + [vmem] * (group + lines + 4),
        out_specs=[vmem] * (group + 1),
        out_shape=[jax.ShapeDtypeStruct((scen, block), F32)] * group
        + [jax.ShapeDtypeStruct((scen + 8, outages), F32)],
        scratch_shapes=[
            pltpu.VMEM((group, table.shape[0], block), F32),
            pltpu.VMEM((scen, outages), F32),
            pltpu.VMEM((outages // 128, scen, 128), F32),
            pltpu.VMEM((2, outages, 128), F32),
            pltpu.VMEM((2, outages, 128), F32),
            pltpu.VMEM((line_rows // 128, scen * 8, 128), F32),
            pltpu.VMEM((outages // 128, (scen + 2) * 8, 128), F32),
            pltpu.VMEM((1, scen * 8, 128), F32),
            pltpu.VMEM((scen, 128), F32),
            pltpu.VMEM((scen, 128), F32),
        ],
        name="outage_stage",
        compiler_params=pltpu.CompilerParams(vmem_limit_bytes=11 << 20),
    )(local, tier, *flows, *picked, turned, energy, table, tier.reshape(1, scen))
    direct, back = results[:group], results[group]
    backs = exchange([back] * lines, "line", lines, 1, lines)
    pieces = pl.pallas_call(
        functools.partial(carry_kernel, group, lines, 2.0 / (outages * buses)),
        in_specs=[smem] + [vmem] * (group + lines + 1),
        out_specs=[vmem] * group,
        out_shape=[jax.ShapeDtypeStruct((scen + 8, block), F32)] * group,
        name="carry",
        compiler_params=pltpu.CompilerParams(vmem_limit_bytes=5 << 20),
    )(local, outage_row, *direct, *backs)
    total = reduce_all(pieces)
    mean_penalty = total[scen, :scen] / (line_rows * lines * outages * buses)
    grads = gather_all(total[:scen])
    (begun,) = spread(order, grads[:1], (0,), None, factors, lines, 40)
    parts = spread(order, grads[1:], away, begun, factors, lines, 40)
    injection_grad = tree_sum(exchange(parts, "line", lines, 1, lines))
    return injection_grad, mean_penalty


def solution(mesh):
    buses = mesh.shape["bus"]
    return jax.shard_map(
        functools.partial(body, mesh.shape["line"], buses),
        mesh=mesh,
        in_specs=(
            P(None, "bus"),
            P("line", "bus"),
            P("line", "bus"),
            P("bus"),
            P(None, "line"),
            P(),
        ),
        out_specs=(P("line", "bus"), P()),
        check_vma=False,
    )
```

```python
import functools

import jax
import jax.numpy as jnp
from jax import lax
from jax.experimental import pallas as pl
from jax.experimental.pallas import tpu as pltpu
from jax.sharding import PartitionSpec as P


SEND_LIMIT = 40
F32 = jnp.float32
BF16 = jnp.bfloat16
NT = (((1,), (1,)), ((), ()))
NN = (((1,), (0,)), ((), ()))


def near(group):
    return lax.rem(lax.axis_index("bus"), group)


def split(x, parts):
    pieces = []
    for _ in range(parts):
        piece = x.astype(BF16)
        pieces.append(piece)
        x = x - piece.astype(F32)
    return pieces


def tile_of(extent, most):
    best = extent
    for size in range(128, most + 1, 128):
        if extent % size == 0:
            best = size
    return best


def tree_sum(values):
    values = list(values)
    while len(values) > 1:
        values = [values[i] + values[i + 1] for i in range(0, len(values), 2)]
    return values[0]


def flow_kernel(group, digits, fresh, inj_ref, factor_ref, *rest):
    outs = rest[: len(digits)]
    if fresh:
        stacked, landed, arrived, raw, ready = rest[len(digits) :]
        first = pltpu.make_async_copy(inj_ref, raw, ready)
        first.start()
    else:
        stacked = inj_ref
        landed, arrived = rest[len(digits) :]
    count, tile, _ = landed.shape
    tiles = count // len(digits)

    def fetch(i, t):
        row = ((near(group) ^ digits[i]) * tiles + t) * tile
        at = i * tiles + t
        return pltpu.make_async_copy(
            factor_ref.at[pl.ds(pl.multiple_of(row, tile), tile), :],
            landed.at[at],
            arrived.at[at],
        )

    for i in range(len(digits)):
        for t in range(tiles):
            fetch(i, t).start()
    scen = stacked.shape[0] // 2
    if fresh:
        first.wait()
        high, low = split(raw[...], 2)
        stacked[:scen, :] = high
        stacked[scen:, :] = low
    for i in range(len(digits)):

        def block(t, carry):
            fetch(i, t).wait()
            total = None
            for part in split(landed[i * tiles + t], 2):
                term = lax.dot_general(
                    part, stacked[...], NT, preferred_element_type=F32
                )
                total = term if total is None else total + term
            total = total.T
            at = pl.ds(pl.multiple_of(t * tile, tile), tile)
            outs[i][:, at] = total[:scen] + total[scen:]
            return carry

        lax.fori_loop(0, tiles, block, 0)


def partial_flows(injections, factors, group, digits, fresh, limit):
    rows, buses = factors.shape
    scen = injections.shape[0] if fresh else injections.shape[0] // 2
    block = rows // group
    tile = tile_of(block, 256)
    count = len(digits) * (block // tile)
    vmem = pl.BlockSpec(memory_space=pltpu.VMEM)
    stacked = [jax.ShapeDtypeStruct((2 * scen, buses), BF16)] if fresh else []
    return pl.pallas_call(
        functools.partial(flow_kernel, group, digits, fresh),
        in_specs=[
            pl.BlockSpec(memory_space=pl.ANY) if fresh else vmem,
            pl.BlockSpec(memory_space=pl.ANY),
        ],
        out_specs=[vmem] * (len(digits) + fresh),
        out_shape=[jax.ShapeDtypeStruct((scen, block), F32)] * len(digits) + stacked,
        scratch_shapes=[
            pltpu.VMEM((count, tile, buses), F32),
            pltpu.SemaphoreType.DMA((count,)),
        ]
        + [pltpu.VMEM((scen, buses), F32), pltpu.SemaphoreType.DMA] * fresh,
        cost_estimate=pl.CostEstimate(
            flops=8 * scen * buses * count * tile,
            bytes_accessed=4 * buses * count * tile,
            transcendentals=0,
        ),
        name="partial_flows",
        compiler_params=pltpu.CompilerParams(vmem_limit_bytes=limit << 20),
    )(injections, factors)


def chosen(group, j, block, outage_row):
    rows = lax.broadcasted_iota(jnp.int32, (block, outage_row.shape[1]), 0)
    start = (lax.axis_index("line") * group + (near(group) ^ j)) * block
    return jnp.where(rows + start == outage_row, 1.0, 0.0).astype(BF16)


def pick_kernel(group, line_ref, *rest):
    flows, out = rest[:group], rest[group]
    scen, block = flows[0].shape
    total = None
    for j in range(group):
        lhs = jnp.concatenate(split(flows[j][...], 3), axis=0)
        part = lax.dot_general(
            lhs,
            chosen(group, j, block, line_ref[...]),
            NN,
            preferred_element_type=F32,
        )
        part = part[:scen] + part[scen : 2 * scen] + part[2 * scen :]
        total = part if total is None else total + part
    out[...] = total


def carry_kernel(group, backs, scale, line_ref, *rest):
    direct = rest[:group]
    parts = rest[group : group + backs]
    outs = rest[group + backs :]
    scen, block = direct[0].shape
    back = tree_sum([part[...] for part in parts])
    lhs = jnp.concatenate(split(back[:scen], 3), axis=0)
    for j in range(group):
        part = lax.dot_general(
            lhs,
            chosen(group, j, block, line_ref[...]),
            NT,
            preferred_element_type=F32,
        )
        part = part[:scen] + part[scen : 2 * scen] + part[2 * scen :]
        outs[j][:scen, :] = scale * (direct[j][...] + part)
        outs[j][scen:, :] = back[scen:, :block]


def turn_kernel(group, factor_ref, turned, energy, terms, landed, arrived):
    lanes = 128
    _, outages, block = turned.shape

    def fetch(j):
        start = pl.multiple_of((near(group) ^ j) * block, lanes)
        return pltpu.make_async_copy(
            factor_ref.at[pl.ds(start, block), :], landed.at[j], arrived.at[j]
        )

    for j in range(group):
        fetch(j).start()
    for j in range(group):
        fetch(j).wait()
        for k in range(outages // lanes):
            cut = slice(k * lanes, (k + 1) * lanes)
            squares = jnp.zeros((lanes, lanes), F32) if j == 0 else energy[cut, :]
            for c in range(block // lanes):
                place = slice(c * lanes, (c + 1) * lanes)
                part = landed[j, place, cut].T
                turned[j, cut, place] = part
                squares = squares + part * part
                for n, term in enumerate(split(part, 3)):
                    terms[n, j, cut, place] = term
            energy[cut, :] = squares


def outage_kernel(group, others, tier_ref, *rest):
    flows = rest[:group]
    picked = rest[group : group + others]
    turned, energy, terms, table_ref, tiers_ref = rest[group + others :][:5]
    rest = rest[group + others + 5 :]
    direct = rest[:group]
    back_ref = rest[group]
    level, all_picked, rows, wide, sums, held, held_back, pen, rows_pen, tier_rows = rest[
        group + 1 :
    ]
    scen, block = flows[0].shape
    outages = energy.shape[0]
    lanes = 128
    cols = block // lanes
    both = 2

    all_picked[...] = tree_sum([ref[...] for ref in picked])
    for j in range(group):
        start = pl.multiple_of((near(group) ^ j) * block, lanes)
        level[j] = 0.4 * table_ref[:, pl.ds(start, block)].astype(F32)

    tiles = outages // lanes

    for k in range(tiles):
        rows[k] = all_picked[:, k * lanes : (k + 1) * lanes]

    def widen(r, s, k):
        at = pl.ds(pl.multiple_of(k * lanes, lanes), lanes)
        row = rows[k, pl.ds(s, 1), :]
        wide[r, at, :] = jnp.broadcast_to(row, (lanes, lanes)).T

    def fold(r, place, k):
        at = pl.ds(pl.multiple_of(k * lanes, lanes), lanes)
        to = pl.ds(pl.multiple_of(place * 8, 8), 8)
        turned_sums = sums[r, at, :].T
        held_back[k, to, :] = tree_sum(
            [turned_sums[8 * i : 8 * (i + 1)] for i in range(lanes // 8)]
        )

    tier_rows[...] = jnp.broadcast_to(tiers_ref[...].astype(F32), (lanes, scen)).T

    def pair(step, carry):
        losses = [None] * both
        for j in range(group):
            lows, highs, limits = [], [], []
            for r in range(both):
                s = step * both + r
                limit = level[j, pl.ds(tier_ref[s], 1), :]
                flow = flows[j][pl.ds(s, 1), :]
                low, high = -limit - flow, limit - flow
                for c in range(cols):
                    cut = slice(c * lanes, (c + 1) * lanes)
                    lows.append(jnp.broadcast_to(low[:, cut], (8, lanes)))
                    highs.append(jnp.broadcast_to(high[:, cut], (8, lanes)))
                    limits.append(limit[:, cut])

            wide_trip = 0 < j < group - 1 and tiles % 2 == 0
            length = 2 * lanes if wide_trip else lanes

            def body(tile, state):
                state = list(state)
                if j == 0:
                    for r in range(both):
                        fold(r, step * both + r, tile)
                for k in range(length // 8):
                    at = pl.ds(pl.multiple_of(tile * length + k * 8, 8), 8)
                    factors = [
                        turned[j, at, c * lanes : (c + 1) * lanes] for c in range(cols)
                    ]
                    for r in range(both):
                        flow = wide[r, at, :]
                        total = flow * energy[at, :] if j == 0 else sums[r, at, :]
                        for c in range(cols):
                            n = r * cols + c
                            raised = jnp.maximum(factors[c] * flow, lows[n])
                            inside = jnp.minimum(raised, highs[n])
                            state[2 * n] = state[2 * n] + raised
                            state[2 * n + 1] = state[2 * n + 1] + inside
                            total = total - inside * factors[c]
                        sums[r, at, :] = total
                if j == group - 1:
                    later = jnp.minimum(step + 1, scen // both - 1)
                    for r in range(both):
                        widen(r, later * both + r, tile)
                return tuple(state)

            init = tuple([jnp.zeros((8, lanes), F32)] * (2 * both * cols))
            state = lax.fori_loop(0, outages // length, body, init)
            for r in range(both):
                at = pl.ds(pl.multiple_of((step * both + r) * 8, 8), 8)
                for c in range(cols):
                    n = r * cols + c
                    raised, inside = state[2 * n], state[2 * n + 1]
                    held[j * cols + c, at, :] = inside
                    loss = limits[n] * (2.0 * raised - inside)
                    losses[r] = loss if losses[r] is None else losses[r] + loss
        for r in range(both):
            at = pl.ds(pl.multiple_of((step * both + r) * 8, 8), 8)
            pen[0, at, :] = losses[r]
        return carry

    sums[...] = jnp.zeros_like(sums)
    for r in range(both):
        for k in range(tiles):
            widen(r, r, k)
    lax.fori_loop(0, scen // both, pair, 0)
    for r in range(both):
        for k in range(tiles):
            fold(r, scen + r, k)

    split_picked = split(all_picked[...], 3)
    for j in range(group):
        every = None
        for n in (2, 1, 0):
            lhs = jnp.concatenate(split_picked[: 3 - n], axis=0)
            part = lax.dot_general(
                lhs, terms[n, j], NN, preferred_element_type=F32
            )
            for i in reversed(range(3 - n)):
                piece = part[i * scen : (i + 1) * scen]
                every = piece if every is None else every + piece
        direct[j][...] = every

    def gathered(ref, step, first, count, skip=0):
        base = (step * 8 + skip) * 8
        whole = [
            tree_sum([ref[i, pl.ds(base + r, 8, stride=8), :] for r in range(8)])
            for i in range(first, first + count)
        ]
        return jnp.concatenate(whole, axis=1)

    def finish(step, carry):
        at = pl.ds(pl.multiple_of(step * 8, 8), 8)
        back = gathered(held_back, step, 0, outages // lanes, both)
        back_ref[at, :] = back
        gain = jnp.sum(all_picked[at, :] * back, axis=1, keepdims=True)
        tiers = tier_rows[at, :1]
        for j in range(group):
            every = direct[j][at, :]
            here = every - gathered(held, step, j * cols, cols)
            limit = jnp.zeros_like(here)
            for t in range(table_ref.shape[0]):
                limit = jnp.where(tiers == t, level[j, t : t + 1, :], limit)
            direct[j][at, :] = here
            gain += jnp.sum(
                flows[j][at, :] * here + limit * every, axis=1, keepdims=True
            )
        loss = jnp.sum(gathered(pen, step, 0, 1), axis=1, keepdims=True)
        rows_pen[at, :] = jnp.broadcast_to(gain - loss, (8, lanes))
        return carry

    lax.fori_loop(0, scen // 8, finish, 0)
    back_ref[scen:, :] = jnp.zeros((back_ref.shape[0] - scen, outages), F32)
    back_ref[scen : scen + 1, :scen] = rows_pen[...].T[:1, :]


def spread_kernel(group, digits, lines, more, *rest):
    grads = rest[: len(digits)]
    factor_ref = rest[len(digits)]
    rest = rest[len(digits) + 1 :]
    if more:
        begun_ref, rest = rest[0], rest[1:]
    outs, (stacked, landed, arrived) = rest[:-3], rest[-3:]
    scen, block = grads[0].shape
    rows = scen // lines
    steps, _, tile = landed.shape

    def fetch(step, i):
        row = pl.multiple_of((near(group) ^ digits[i]) * block, 8)
        cut = pl.ds(pl.multiple_of(step * tile, tile), tile)
        return pltpu.make_async_copy(
            factor_ref.at[pl.ds(row, block), cut],
            landed.at[step, pl.ds(i * block, block), :],
            arrived.at[step, i],
        )

    for step in range(steps):
        for i in range(len(digits)):
            fetch(step, i).start()
    for j in range(len(digits)):
        for i in range(lines):
            place = (lax.axis_index("line") ^ i) * rows
            at = pl.ds(pl.multiple_of(place, 8), rows)
            high, low = split(grads[j][at, :], 2)
            stacked[j, i * rows : (i + 1) * rows, :] = high.astype(F32)
            stacked[j, scen + i * rows : scen + (i + 1) * rows, :] = low.astype(F32)

    def piece(step, carry):
        cut = pl.ds(pl.multiple_of(step * tile, tile), tile)
        total = None
        for j in range(len(digits)):
            fetch(step, j).wait()
        for j in range(len(digits)):
            lhs = stacked[j].astype(BF16)
            for part in split(landed[step, j * block : (j + 1) * block, :], 2):
                term = lax.dot_general(lhs, part, NN, preferred_element_type=F32)
                total = term if total is None else total + term
        total = total[:scen] + total[scen:]
        if more:
            total = total + begun_ref[:, cut]
        count = scen // len(outs)
        for i in range(len(outs)):
            outs[i][:, cut] = total[i * count : (i + 1) * count]
        return carry

    lax.fori_loop(0, steps, piece, 0)


def spread(group, grads, digits, begun, factors, lines, limit):
    scen, block = grads[0].shape
    buses = factors.shape[1]
    tile = tile_of(buses, 256)
    steps = buses // tile
    more = begun is not None
    outs = lines if more else 1
    vmem = pl.BlockSpec(memory_space=pltpu.VMEM)
    return pl.pallas_call(
        functools.partial(spread_kernel, group, digits, lines, more),
        in_specs=[vmem] * len(grads)
        + [pl.BlockSpec(memory_space=pl.ANY)]
        + [vmem] * more,
        out_specs=[vmem] * outs,
        out_shape=[jax.ShapeDtypeStruct((scen // outs, buses), F32)] * outs,
        scratch_shapes=[
            pltpu.VMEM((len(grads), 2 * scen, block), F32),
            pltpu.VMEM((steps, len(grads) * block, tile), F32),
            pltpu.SemaphoreType.DMA((steps, len(grads))),
        ],
        cost_estimate=pl.CostEstimate(
            flops=8 * scen * buses * block * len(grads),
            bytes_accessed=4 * buses * block * len(grads),
            transcendentals=0,
        ),
        name="spread",
        compiler_params=pltpu.CompilerParams(vmem_limit_bytes=limit << 20),
    )(*grads, factors, *([begun] if more else []))


def exchange(values, axis, size, stride, count):
    got = [values[0]]
    for j in range(1, count):
        pairs = [(d, d ^ (j * stride)) for d in range(size)]
        got.append(lax.ppermute(values[j], axis, pairs))
    return got


def body(lines, buses, *args):
    return staged(lines, buses, *args)


def staged(lines, buses, injections, factors, outage_factors, outage_line, table, tier):
    scen = injections.shape[0]
    line_rows = factors.shape[0]
    outages = outage_factors.shape[1]
    group = min(4, buses)
    depth = buses // group
    block = line_rows // group
    outage_row = outage_line.reshape(1, outages)
    smem = pl.BlockSpec(memory_space=pltpu.SMEM)
    vmem = pl.BlockSpec(memory_space=pltpu.VMEM)
    away = tuple(range(1, group))

    def reduce_all(pieces):
        mine = tree_sum(exchange(pieces, "bus", buses, 1, group))
        return tree_sum(exchange([mine] * depth, "bus", buses, group, depth))

    def gather_all(mine):
        return exchange([mine] * group, "bus", buses, 1, group)

    *sent, stacked = partial_flows(
        injections, factors, group, away, True, SEND_LIMIT
    )
    own = partial_flows(stacked, factors, group, (0,), False, 40)
    flows = gather_all(reduce_all([*own, *sent]))
    turned, energy, terms = pl.pallas_call(
        functools.partial(turn_kernel, group),
        in_specs=[pl.BlockSpec(memory_space=pl.ANY)],
        out_specs=[vmem] * 3,
        out_shape=[
            jax.ShapeDtypeStruct((group, outages, block), F32),
            jax.ShapeDtypeStruct((outages, 128), F32),
            jax.ShapeDtypeStruct((3, group, outages, block), BF16),
        ],
        scratch_shapes=[
            pltpu.VMEM((group, block, outages), F32),
            pltpu.SemaphoreType.DMA((group,)),
        ],
        cost_estimate=pl.CostEstimate(
            flops=2 * line_rows * outages,
            bytes_accessed=12 * line_rows * outages,
            transcendentals=0,
        ),
        name="turn",
        compiler_params=pltpu.CompilerParams(vmem_limit_bytes=6 << 20),
    )(outage_factors)
    picked = pl.pallas_call(
        functools.partial(pick_kernel, group),
        in_specs=[vmem] * (group + 1),
        out_specs=vmem,
        out_shape=jax.ShapeDtypeStruct((scen, outages), F32),
        name="pick",
        compiler_params=pltpu.CompilerParams(vmem_limit_bytes=5 << 20),
    )(outage_row, *flows)
    picked = exchange([picked] * lines, "line", lines, 1, lines)
    results = pl.pallas_call(
        functools.partial(outage_kernel, group, lines),
        in_specs=[smem] + [vmem] * (group + lines + 5),
        out_specs=[vmem] * (group + 1),
        out_shape=[jax.ShapeDtypeStruct((scen, block), F32)] * group
        + [jax.ShapeDtypeStruct((scen + 8, outages), F32)],
        scratch_shapes=[
            pltpu.VMEM((group, table.shape[0], block), F32),
            pltpu.VMEM((scen, outages), F32),
            pltpu.VMEM((outages // 128, scen, 128), F32),
            pltpu.VMEM((2, outages, 128), F32),
            pltpu.VMEM((2, outages, 128), F32),
            pltpu.VMEM((line_rows // 128, scen * 8, 128), F32),
            pltpu.VMEM((outages // 128, (scen + 2) * 8, 128), F32),
            pltpu.VMEM((1, scen * 8, 128), F32),
            pltpu.VMEM((scen, 128), F32),
            pltpu.VMEM((scen, 128), F32),
        ],
        name="outage_stage",
        compiler_params=pltpu.CompilerParams(vmem_limit_bytes=11 << 20),
    )(tier, *flows, *picked, turned, energy, terms, table, tier.reshape(1, scen))
    direct, back = results[:group], results[group]
    backs = exchange([back] * lines, "line", lines, 1, lines)
    pieces = pl.pallas_call(
        functools.partial(carry_kernel, group, lines, 2.0 / (outages * buses)),
        in_specs=[vmem] * (group + lines + 1),
        out_specs=[vmem] * group,
        out_shape=[jax.ShapeDtypeStruct((scen + 8, block), F32)] * group,
        name="carry",
        compiler_params=pltpu.CompilerParams(vmem_limit_bytes=5 << 20),
    )(outage_row, *direct, *backs)
    total = reduce_all(pieces)
    mean_penalty = total[scen, :scen] / (line_rows * lines * outages * buses)
    grads = gather_all(total[:scen])
    (begun,) = spread(group, grads[:1], (0,), None, factors, lines, 40)
    parts = spread(group, grads[1:], away, begun, factors, lines, 40)
    injection_grad = tree_sum(exchange(parts, "line", lines, 1, lines))
    return injection_grad, mean_penalty


def solution(mesh):
    buses = mesh.shape["bus"]
    return jax.shard_map(
        functools.partial(body, mesh.shape["line"], buses),
        mesh=mesh,
        in_specs=(
            P(None, "bus"),
            P("line", "bus"),
            P("line", "bus"),
            P("bus"),
            P(None, "line"),
            P(),
        ),
        out_specs=(P("line", "bus"), P()),
        check_vma=False,
    )
```
